32 devices in a mesh: dp: 4 (over x, core), ctx: 2 (over y), tp: 4 (over z).
Axes of the slice: x: 2, y: 2, z: 4, core: 2. Of those that a mesh axis runs over, the one named last changes fastest.
Arguments:
- out_grad: bfloat16 [4096, 4096], P(('dp', 'ctx', 'tp')), may hold values from -6 to 6
- expert_ids: int32 [4096, 1], P(('dp', 'ctx', 'tp')), may hold values from 0 to 3
- gate_weight: float32 [4096, 1], P(('dp', 'ctx', 'tp')), may hold values from 0.2 to 1
- hidden_saved: bfloat16 [4, 4, 256, 1536], P('dp', 'tp', None, 'ctx'), may hold values from -1 to 1
- down_weight: bfloat16 [4, 1536, 4096], P('tp', 'ctx'), may hold values from -0.15625 to 0.15625
Outputs:
- hidden_grad: bfloat16 [4, 4, 256, 1536], P('dp', 'tp', None, 'ctx')
- weight_grad: bfloat16 [4, 1536, 4096], P('tp', 'ctx', 'dp')
The draws below stay inside these ranges and needn't reach their ends.
All inputs are finite; a program needn't handle non-finite values.
Results may differ from the reference program's by a relative error of at most 0.013.
Values may be sent and summed in bfloat16 or wider, within the bound.
A program may use at most 64 MiB of HBM per device.

```python
import jax
import jax.numpy as jnp
from jax import lax

D = 4096
FF = 1536
TOK_DEV = 128
EXPERTS = 4
CAP = 32
SLOTS = 256
TOKENS = 4096
N_DP = 4
N_CTX = 2
N_TP = 4


def block_levels(stream_key, dims, cuts, least, top_value):
    factor_of, own = 1.0, jax.random.fold_in(stream_key, 6)
    for axis_at, shards_of in cuts:
        heights = jnp.exp(jax.random.uniform(jax.random.fold_in(own, axis_at), (shards_of,), jnp.float32, least / len(cuts), top_value / len(cuts)))
        factor_of = factor_of * jnp.repeat(heights, dims[axis_at] // shards_of).reshape([-1 if axis == axis_at else 1 for axis in range(len(dims))])
    return factor_of


def choose_distinct(key, rows, amount, top, lift):
    ranking = jax.random.permutation(jax.random.fold_in(key, 1), amount)
    boost = ranking
    for power in range(3):
        boost = boost * boost // amount
    boost = boost * lift // amount
    chance = jax.random.randint(jax.random.fold_in(key, 2), (rows, amount), 0, 4096) + boost
    fixed_rows = jax.random.permutation(jax.random.fold_in(key, 3), rows)[jnp.arange(amount) % rows]
    chance = jnp.where(jnp.arange(rows)[:, None] == fixed_rows[None, :], 1 << 14, chance)
    merit = chance * amount + jnp.arange(amount)
    return lax.top_k(merit.astype(jnp.int32), top)[1].astype(jnp.int32)


def centred(own_key, extent, scale, most, shards=(), kind=jnp.bfloat16):
    level = block_levels(own_key, extent, shards, -0.22, 0.18) if shards else 1.0
    entries = jax.random.normal(own_key, extent, jnp.float32) * scale * level
    return jnp.minimum(jnp.maximum(entries, -most), most).astype(kind)


def setup_inputs(seed: int = 0) -> dict:
    splits = jax.random.split(jax.random.key(seed), 6)
    out_grad = centred(splits[0], (TOKENS, D), 1.0, 6.0, ((0, 32),))
    expert_ids = choose_distinct(splits[1], TOKENS, EXPERTS, 1, 4096)
    gate_weight = jnp.clip(0.2 + 0.8 * jax.random.uniform(splits[2], (TOKENS, 1), jnp.float32) ** block_levels(splits[2], (TOKENS, 1), ((0, 32),), -0.2, 0.2), 0.2, 1.0)
    hidden_saved = centred(splits[3], (N_DP, EXPERTS, SLOTS, FF), (2.0 / (SLOTS * N_DP) ** 0.5), 1.0, ((0, 4), (1, 4), (3, 2)))
    down_weight = centred(splits[4], (EXPERTS, FF, D), FF ** -0.5, 0.15625, ((0, 4), (1, 2)))
    return dict(out_grad=out_grad, expert_ids=expert_ids, gate_weight=gate_weight, hidden_saved=hidden_saved, down_weight=down_weight)


def place(pieces):
    grad_rows, gates, choice_rows = pieces
    group = N_CTX * N_TP
    onehot = (choice_rows[:, :, None] == jnp.arange(EXPERTS, dtype=jnp.int32)[None, None, :]).astype(jnp.int32)
    before = jnp.cumsum(onehot, axis=1) - onehot
    slot_index = jnp.sum(before * onehot, axis=2).astype(jnp.int32)
    source = jnp.arange(group, dtype=jnp.int32)[:, None]
    slot_row = jnp.where(slot_index < CAP, source * CAP + slot_index, group * CAP).astype(jnp.int32)
    routed = (gates * grad_rows.astype(jnp.float32)).astype(jnp.bfloat16).reshape(group, TOK_DEV, D)
    empty = jnp.zeros((EXPERTS, group * CAP, D), jnp.bfloat16)
    return empty.at[choice_rows, slot_row].set(routed, mode="drop")


def expert_work(pieces):
    rows_in, saved_rows, weight = pieces
    rows_wide = rows_in.astype(jnp.float32)
    hidden_grad = jnp.einsum("nrd,fd->nrf", rows_wide, weight.astype(jnp.float32)).astype(jnp.bfloat16)
    partial_value = jnp.einsum("nrf,nrd->nfd", saved_rows.astype(jnp.float32), rows_wide).astype(jnp.bfloat16)
    partial_value = lax.optimization_barrier(partial_value)
    total = jnp.sum(partial_value.astype(jnp.float32), axis=0).astype(jnp.bfloat16)
    return hidden_grad, total


def reference(out_grad, expert_ids, gate_weight, hidden_saved, down_weight):
    group = N_CTX * N_TP
    dispatched = lax.map(place, (out_grad.reshape(N_DP, group * TOK_DEV, D), gate_weight.reshape(N_DP, group * TOK_DEV, 1), expert_ids.reshape(N_DP, group, TOK_DEV)))
    hidden_grad, weight_grad = lax.map(expert_work, (jnp.swapaxes(dispatched, 0, 1), jnp.swapaxes(hidden_saved, 0, 1), down_weight))
    return jnp.swapaxes(hidden_grad, 0, 1), weight_grad
```

```python
import functools

import jax
import jax.numpy as jnp
from jax import lax
from jax.experimental import pallas as pl
from jax.experimental.pallas import tpu as pltpu
from jax.sharding import PartitionSpec as P

MESH = pl.DeviceIdType.MESH
RELAY = ()
ROWS_PER_TILE = 16
LANES = 128


def plain(out_grad, expert_ids, gate_weight, hidden_saved, down_weight):
    experts = lax.axis_size("tp")
    width = out_grad.shape[1]
    slots_all = hidden_saved.shape[2]
    capacity = slots_all // (lax.axis_size("ctx") * experts)
    choice_rows = expert_ids[:, 0]
    onehot = (choice_rows[:, None] == jnp.arange(experts, dtype=jnp.int32)[None, :]).astype(
        jnp.int32
    )
    before = jnp.cumsum(onehot, axis=0) - onehot
    slot_index = jnp.sum(before * onehot, axis=1)
    target = jnp.arange(experts * capacity, dtype=jnp.int32)
    select = (
        (choice_rows[None, :] == (target // capacity)[:, None])
        & (slot_index[None, :] == (target % capacity)[:, None])
    ).astype(jnp.bfloat16)
    routed = (gate_weight * out_grad.astype(jnp.float32)).astype(jnp.bfloat16)
    outgoing = jnp.dot(select, routed, preferred_element_type=jnp.float32).astype(jnp.bfloat16)
    outgoing = outgoing.reshape(experts, capacity, width)
    incoming = lax.all_to_all(outgoing, "tp", split_axis=0, concat_axis=0, tiled=True)
    incoming = incoming.reshape(experts * capacity, width)
    group_rows = lax.all_gather(incoming, "ctx", axis=0, tiled=True)
    hidden_grad = jnp.einsum(
        "rd,fd->rf", group_rows, down_weight[0], preferred_element_type=jnp.float32
    )
    partial_value = jnp.einsum(
        "rf,rd->fd", hidden_saved[0, 0], group_rows, preferred_element_type=jnp.float32
    )
    rounded = lax.optimization_barrier(partial_value.astype(jnp.bfloat16)).astype(jnp.float32)
    summed = lax.psum_scatter(rounded.astype(jnp.bfloat16), "dp", scatter_dimension=1, tiled=True)
    return (hidden_grad.astype(jnp.bfloat16)[None, None], summed[None])


def kernel(
    sizes, ids_ref, gate_ref, og_hbm, hs_hbm, dw_hbm, hg_ref, wg_ref,
    ogb, wbuf, outb, disp, gath, hid, hgacc, wgacc,
    load_sem, zs, zr, ys, yr, ps, pr, hs, hr,
):
    n_dp, n_ctx, n_tp, cap = sizes
    half = n_dp // 2
    rows = n_tp * cap
    width = ogb.shape[2]
    slots = n_ctx * rows
    ff = hid.shape[2]
    last = n_dp - 1
    r, c, t = lax.axis_index("dp"), lax.axis_index("ctx"), lax.axis_index("tp")
    hi, lo = r // 2, r % 2

    steps = [(a, b) for a in range(1, half) for b in (0, 1)] + [(0, 1), (0, 0)]

    def replica(a, b):
        return lax.rem(hi + a, half) * 2 + lax.rem(lo + b, 2)

    dest = [replica(a, b) for a, b in steps]

    og_loads, w_loads = [], []
    for k in range(n_dp):
        cols = pl.ds(pl.multiple_of(dest[k] * width, LANES), width)
        cp = pltpu.make_async_copy(og_hbm.at[:, cols], ogb.at[k], load_sem.at[0, k])
        cp.start()
        og_loads.append(cp)
    hid_load = pltpu.make_async_copy(hs_hbm, hid.at[last], load_sem.at[2, 0])
    hid_load.start()
    for k in range(n_dp):
        cols = pl.ds(pl.multiple_of(dest[k] * width, LANES), width)
        cp = pltpu.make_async_copy(dw_hbm.at[:, cols], wbuf.at[k], load_sem.at[1, k])
        cp.start()
        w_loads.append(cp)

    barrier = pltpu.get_barrier_semaphore()
    peers = [(r, c, lax.rem(t + d, n_tp)) for d in range(1, n_tp)]
    peers += [(r, lax.rem(c + d, n_ctx), t) for d in range(1, n_ctx)]
    peers += [(dest[k], c, t) for k in range(n_dp - 1)]
    for peer in peers:
        pl.semaphore_signal(barrier, inc=1, device_id=peer, device_id_type=MESH)

    tokens = ids_ref.shape[0]
    lane = lax.broadcasted_iota(jnp.int32, (tokens, rows), 1)
    lane_expert = lane // cap
    lane_slot = (lane - lane_expert * cap).astype(jnp.float32)
    mine = ids_ref[...] == lane_expert
    onehot = jnp.where(mine, 1.0, 0.0)
    earlier = (
        lax.broadcasted_iota(jnp.int32, (tokens, tokens), 1)
        < lax.broadcasted_iota(jnp.int32, (tokens, tokens), 0)
    )
    before = jnp.dot(
        jnp.where(earlier, 1.0, 0.0).astype(jnp.bfloat16),
        onehot.astype(jnp.bfloat16),
        preferred_element_type=jnp.float32,
    )
    select = jnp.where(before == lane_slot, onehot, 0.0).T.astype(jnp.bfloat16)
    gate = gate_ref[...]

    started = []

    def send(src, dst, ssem, rsem, device):
        cp = pltpu.make_async_remote_copy(
            src_ref=src, dst_ref=dst, send_sem=ssem, recv_sem=rsem,
            device_id=device, device_id_type=MESH,
        )
        cp.start()
        started.append(cp)
        return cp

    hid_recv = [None] * n_dp
    z_recv = []
    own_rows = pl.ds(pl.multiple_of(t * cap, cap), cap)
    for k in range(n_dp):
        og_loads[k].wait()
        routed = (gate * ogb[k].astype(jnp.float32)).astype(jnp.bfloat16)
        outb[k] = jnp.dot(select, routed, preferred_element_type=jnp.float32).astype(jnp.bfloat16)
        if k == 0:
            pl.semaphore_wait(barrier, len(peers))
        copies = []
        for d in range(1, n_tp):
            to = lax.rem(t + d, n_tp)
            src = outb.at[k, pl.ds(pl.multiple_of(to * cap, cap), cap)]
            copies.append(
                send(src, disp.at[k, c, own_rows], zs.at[k, d - 1], zr.at[k, d - 1], (r, c, to))
            )
        z_recv.append(copies)
        disp[k, c, own_rows, :] = outb[k, own_rows, :]
        if k == 0:
            for a in range(1, half):
                s = 2 * (a - 1)
                hid_recv[s] = send(hs_hbm, hid.at[s], hs.at[s], hr.at[s], (dest[s], c, t))
            s = n_dp - 2
            hid_recv[s] = send(hs_hbm, hid.at[s], hs.at[s], hr.at[s], (dest[s], c, t))

    y_recv = [None] * n_dp
    p_recv = [[None] * n_ctx for _ in range(n_dp)]

    def relay_hidden(a):
        s = 2 * (a - 1)
        hid_recv[s].wait_recv()
        hid_recv[s + 1] = send(
            hid.at[s], hid.at[s + 1], hs.at[s + 1], hr.at[s + 1], (dest[n_dp - 2], c, t)
        )

    def hidden_part(k):
        w_loads[k].wait()
        part = lax.dot_general(
            disp[k].reshape(slots, width), wbuf[k], (((1,), (1,)), ((), ())),
            preferred_element_type=jnp.float32,
        )
        if k == 0:
            hgacc[...] = part
        elif k < last:
            hgacc[...] += part
        else:
            hg_ref[...] = (hgacc[...] + part).astype(hg_ref.dtype)

    def weight_part(k, rows_in, first, final):
        tile = 256 if ff % 256 == 0 else LANES
        for f in range(0, ff, tile):
            part = lax.dot_general(
                hid[k, :, f : f + tile], rows_in, (((0,), (0,)), ((), ())),
                preferred_element_type=jnp.float32,
            )
            if not first:
                part = wgacc[f : f + tile, :] + part
            if final:
                wg_ref[f : f + tile, :] = part.astype(wg_ref.dtype)
            else:
                wgacc[f : f + tile, :] = part

    def finish_y(k):
        for d in range(1, n_ctx):
            y_recv[k][d - 1].wait_recv()
            if k < last and k not in RELAY:
                other = lax.rem(c + d, n_ctx)
                p_recv[k][d] = send(
                    disp.at[k, other], gath.at[k, other], ps.at[k, d], pr.at[k, d], (dest[k], c, t)
                )
        hidden_part(k)

    def relay_piece(k):
        p_recv[k][0].wait_recv()
        for d in range(1, n_ctx):
            to = lax.rem(c + n_ctx - d, n_ctx)
            p_recv[k][d] = send(gath.at[k, c], gath.at[k, c], ps.at[k, d], pr.at[k, d], (r, to, t))

    for k in range(n_dp):
        for cp in z_recv[k]:
            cp.wait_recv()
        y_recv[k] = []
        if k < last:
            p_recv[k][0] = send(
                disp.at[k, c], gath.at[k, c], ps.at[k, 0], pr.at[k, 0], (dest[k], c, t)
            )
        for d in range(1, n_ctx):
            to = lax.rem(c + n_ctx - d, n_ctx)
            y_recv[k].append(
                send(disp.at[k, c], disp.at[k, c], ys.at[k, d - 1], yr.at[k, d - 1], (r, to, t))
            )
        if k >= 1:
            finish_y(k - 1)
        if 1 <= k < half:
            relay_hidden(k)
        if k >= 2 and (k - 2) in RELAY:
            relay_piece(k - 2)
    for k in range(last - 1, last):
        if k in RELAY:
            relay_piece(k)
    finish_y(last)

    hid_load.wait()
    weight_part(last, disp[last].reshape(slots, width), True, n_dp == 1)
    arrive = [n_dp - 2] + list(range(n_dp - 2))
    for at, k in enumerate(arrive):
        if k >= n_dp - 2 or k % 2 == 1:
            hid_recv[k].wait_recv()
        for cp in p_recv[k][1:] if k in RELAY else p_recv[k]:
            cp.wait_recv()
        weight_part(k, gath[k].reshape(slots, width), False, at == len(arrive) - 1)
    for cp in started:
        cp.wait_send()


def fused(sizes, out_grad, expert_ids, gate_weight, hidden_saved, down_weight):
    n_dp, n_ctx, n_tp, cap = sizes
    tokens, d_model = out_grad.shape
    width = d_model // n_dp
    rows = n_tp * cap
    slots, ff = hidden_saved.shape[2:]
    bf, dma = jnp.bfloat16, pltpu.SemaphoreType.DMA
    vmem, hbm = pl.BlockSpec(memory_space=pltpu.VMEM), pl.BlockSpec(memory_space=pl.ANY)
    hidden_grad, weight_grad = pl.pallas_call(
        functools.partial(kernel, sizes),
        out_shape=(
            jax.ShapeDtypeStruct((slots, ff), bf),
            jax.ShapeDtypeStruct((ff, width), bf),
        ),
        in_specs=[vmem, vmem, hbm, hbm, hbm],
        out_specs=(vmem, vmem),
        scratch_shapes=[
            pltpu.VMEM((n_dp, tokens, width), bf),
            pltpu.VMEM((n_dp, ff, width), bf),
            pltpu.VMEM((n_dp, rows, width), bf),
            pltpu.VMEM((n_dp, n_ctx, rows, width), bf),
            pltpu.VMEM((n_dp - 1, n_ctx, rows, width), bf),
            pltpu.VMEM((n_dp, slots, ff), bf),
            pltpu.VMEM((slots, ff), jnp.float32),
            pltpu.VMEM((ff, width), jnp.float32),
            dma((3, n_dp)),
            dma((n_dp, n_tp)),
            dma((n_dp, n_tp)),
            dma((n_dp, n_ctx)),
            dma((n_dp, n_ctx)),
            dma((n_dp, n_ctx)),
            dma((n_dp, n_ctx)),
            dma((n_dp,)),
            dma((n_dp,)),
        ],
        compiler_params=pltpu.CompilerParams(collective_id=0, has_side_effects=True),
    )(expert_ids, gate_weight, out_grad, hidden_saved[0, 0], down_weight[0])
    return hidden_grad[None, None], weight_grad[None]


def per_device(out_grad, expert_ids, gate_weight, hidden_saved, down_weight):
    n_dp, n_ctx, n_tp = (lax.axis_size(name) for name in ("dp", "ctx", "tp"))
    slots, ff = hidden_saved.shape[2:]
    cap = slots // (n_ctx * n_tp)
    args = (out_grad, expert_ids, gate_weight, hidden_saved, down_weight)
    tiled = cap % ROWS_PER_TILE == 0 and ff % LANES == 0 and n_dp % 2 == 0
    if tiled and out_grad.shape[1] % (n_dp * LANES) == 0:
        return fused((n_dp, n_ctx, n_tp, cap), *args)
    return plain(*args)


def solution(mesh):
    placed = (
        P(("dp", "ctx", "tp"), None),
        P(("dp", "ctx", "tp"), None),
        P(("dp", "ctx", "tp"), None),
        P("dp", "tp", None, "ctx"),
        P("tp", "ctx", None),
    )
    return jax.shard_map(
        per_device,
        mesh=mesh,
        in_specs=placed,
        out_specs=(P("dp", "tp", None, "ctx"), P("tp", "ctx", "dp")),
        check_vma=False,
    )
```

```python
import functools

import jax
import jax.numpy as jnp
from jax import lax
from jax.experimental import pallas as pl
from jax.experimental.pallas import tpu as pltpu
from jax.sharding import PartitionSpec as P

MESH = pl.DeviceIdType.MESH
RELAY = ()
ROWS_PER_TILE = 16
LANES = 128


def plain(out_grad, expert_ids, gate_weight, hidden_saved, down_weight):
    experts = lax.axis_size("tp")
    width = out_grad.shape[1]
    slots_all = hidden_saved.shape[2]
    capacity = slots_all // (lax.axis_size("ctx") * experts)
    choice_rows = expert_ids[:, 0]
    onehot = (choice_rows[:, None] == jnp.arange(experts, dtype=jnp.int32)[None, :]).astype(
        jnp.int32
    )
    before = jnp.cumsum(onehot, axis=0) - onehot
    slot_index = jnp.sum(before * onehot, axis=1)
    target = jnp.arange(experts * capacity, dtype=jnp.int32)
    select = (
        (choice_rows[None, :] == (target // capacity)[:, None])
        & (slot_index[None, :] == (target % capacity)[:, None])
    ).astype(jnp.bfloat16)
    routed = (gate_weight * out_grad.astype(jnp.float32)).astype(jnp.bfloat16)
    outgoing = jnp.dot(select, routed, preferred_element_type=jnp.float32).astype(jnp.bfloat16)
    outgoing = outgoing.reshape(experts, capacity, width)
    incoming = lax.all_to_all(outgoing, "tp", split_axis=0, concat_axis=0, tiled=True)
    incoming = incoming.reshape(experts * capacity, width)
    group_rows = lax.all_gather(incoming, "ctx", axis=0, tiled=True)
    hidden_grad = jnp.einsum(
        "rd,fd->rf", group_rows, down_weight[0], preferred_element_type=jnp.float32
    )
    partial_value = jnp.einsum(
        "rf,rd->fd", hidden_saved[0, 0], group_rows, preferred_element_type=jnp.float32
    )
    rounded = lax.optimization_barrier(partial_value.astype(jnp.bfloat16)).astype(jnp.float32)
    summed = lax.psum_scatter(rounded.astype(jnp.bfloat16), "dp", scatter_dimension=1, tiled=True)
    return (hidden_grad.astype(jnp.bfloat16)[None, None], summed[None])


def kernel(
    sizes, ids_ref, gate_ref, og_hbm, hs_hbm, dw_hbm, hg_ref, wg_ref,
    ogb, wbuf, outb, disp, gath, hid, hgacc, wgacc,
    load_sem, zs, zr, ys, yr, ps, pr, hs, hr,
):
    n_dp, n_ctx, n_tp, cap = sizes
    half = n_dp // 2
    rows = n_tp * cap
    width = ogb.shape[2]
    slots = n_ctx * rows
    ff = hid.shape[2]
    last = n_dp - 1
    r, c, t = lax.axis_index("dp"), lax.axis_index("ctx"), lax.axis_index("tp")
    hi, lo = r // 2, r % 2

    steps = [(a, b) for a in range(1, half) for b in (0, 1)] + [(0, 1), (0, 0)]

    def replica(a, b):
        return lax.rem(hi + a, half) * 2 + lax.rem(lo + b, 2)

    dest = [replica(a, b) for a, b in steps]

    og_loads, w_loads = [], []
    for k in range(n_dp):
        cols = pl.ds(pl.multiple_of(dest[k] * width, LANES), width)
        cp = pltpu.make_async_copy(og_hbm.at[:, cols], ogb.at[k], load_sem.at[0, k])
        cp.start()
        og_loads.append(cp)
    hid_load = pltpu.make_async_copy(hs_hbm, hid.at[last], load_sem.at[2, 0])
    hid_load.start()
    for k in range(n_dp):
        cols = pl.ds(pl.multiple_of(dest[k] * width, LANES), width)
        cp = pltpu.make_async_copy(dw_hbm.at[:, cols], wbuf.at[k], load_sem.at[1, k])
        cp.start()
        w_loads.append(cp)

    barrier = pltpu.get_barrier_semaphore()
    peers = [(r, c, lax.rem(t + d, n_tp)) for d in range(1, n_tp)]
    peers += [(r, lax.rem(c + d, n_ctx), t) for d in range(1, n_ctx)]
    peers += [(dest[k], c, t) for k in range(n_dp - 1)]
    for peer in peers:
        pl.semaphore_signal(barrier, inc=1, device_id=peer, device_id_type=MESH)

    tokens = ids_ref.shape[1]
    row = lax.broadcasted_iota(jnp.int32, (rows, tokens), 0)
    row_expert = row // cap
    row_slot = (row - row_expert * cap).astype(jnp.float32)
    onehot = jnp.where(ids_ref[...] == row_expert, 1.0, 0.0)
    earlier = (
        lax.broadcasted_iota(jnp.int32, (tokens, tokens), 0)
        < lax.broadcasted_iota(jnp.int32, (tokens, tokens), 1)
    )
    before = jnp.dot(
        onehot.astype(jnp.bfloat16),
        jnp.where(earlier, 1.0, 0.0).astype(jnp.bfloat16),
        preferred_element_type=jnp.float32,
    )
    select = jnp.where(before == row_slot, onehot, 0.0).astype(jnp.bfloat16)
    gate = jnp.broadcast_to(gate_ref[...], (tokens, tokens)).T[:, :1]

    started = []

    def send(src, dst, ssem, rsem, device):
        cp = pltpu.make_async_remote_copy(
            src_ref=src, dst_ref=dst, send_sem=ssem, recv_sem=rsem,
            device_id=device, device_id_type=MESH,
        )
        cp.start()
        started.append(cp)
        return cp

    hid_recv = [None] * n_dp
    pl.semaphore_wait(barrier, len(peers))
    for s in [2 * a for a in range(half - 1)] + [n_dp - 2]:
        hid_recv[s] = send(hs_hbm, hid.at[s], hs.at[s], hr.at[s], (dest[s], c, t))
    z_recv = []
    own_rows = pl.ds(pl.multiple_of(t * cap, cap), cap)
    for k in range(n_dp):
        og_loads[k].wait()
        routed = (gate * ogb[k].astype(jnp.float32)).astype(jnp.bfloat16)
        outb[k] = jnp.dot(select, routed, preferred_element_type=jnp.float32).astype(jnp.bfloat16)
        copies = []
        for d in range(1, n_tp):
            to = lax.rem(t + d, n_tp)
            src = outb.at[k, pl.ds(pl.multiple_of(to * cap, cap), cap)]
            copies.append(
                send(src, disp.at[k, c, own_rows], zs.at[k, d - 1], zr.at[k, d - 1], (r, c, to))
            )
        z_recv.append(copies)
        disp[k, c, own_rows, :] = outb[k, own_rows, :]

    y_recv = [None] * n_dp
    p_recv = [[None] * n_ctx for _ in range(n_dp)]

    def relay_hidden(a):
        s = 2 * (a - 1)
        hid_recv[s].wait_recv()
        hid_recv[s + 1] = send(
            hid.at[s], hid.at[s + 1], hs.at[s + 1], hr.at[s + 1], (dest[n_dp - 2], c, t)
        )

    def hidden_part(k):
        w_loads[k].wait()
        part = lax.dot_general(
            disp[k].reshape(slots, width), wbuf[k], (((1,), (1,)), ((), ())),
            preferred_element_type=jnp.float32,
        )
        if k == 0:
            hgacc[...] = part
        elif k < last:
            hgacc[...] += part
        else:
            hg_ref[...] = (hgacc[...] + part).astype(hg_ref.dtype)

    def weight_part(k, rows_in, first, final):
        tile = 256 if ff % 256 == 0 else LANES
        for f in range(0, ff, tile):
            part = lax.dot_general(
                hid[k, :, f : f + tile], rows_in, (((0,), (0,)), ((), ())),
                preferred_element_type=jnp.float32,
            )
            if not first:
                part = wgacc[f : f + tile, :] + part
            if final:
                wg_ref[f : f + tile, :] = part.astype(wg_ref.dtype)
            else:
                wgacc[f : f + tile, :] = part

    def finish_y(k):
        for d in range(1, n_ctx):
            y_recv[k][d - 1].wait_recv()
            if k < last and k not in RELAY:
                other = lax.rem(c + d, n_ctx)
                p_recv[k][d] = send(
                    disp.at[k, other], gath.at[k, other], ps.at[k, d], pr.at[k, d], (dest[k], c, t)
                )
        hidden_part(k)

    def relay_piece(k):
        p_recv[k][0].wait_recv()
        for d in range(1, n_ctx):
            to = lax.rem(c + n_ctx - d, n_ctx)
            p_recv[k][d] = send(gath.at[k, c], gath.at[k, c], ps.at[k, d], pr.at[k, d], (r, to, t))

    for k in range(n_dp):
        for cp in z_recv[k]:
            cp.wait_recv()
        y_recv[k] = []
        if k < last:
            p_recv[k][0] = send(
                disp.at[k, c], gath.at[k, c], ps.at[k, 0], pr.at[k, 0], (dest[k], c, t)
            )
        for d in range(1, n_ctx):
            to = lax.rem(c + n_ctx - d, n_ctx)
            y_recv[k].append(
                send(disp.at[k, c], disp.at[k, c], ys.at[k, d - 1], yr.at[k, d - 1], (r, to, t))
            )
        if k >= 1:
            finish_y(k - 1)
        if 1 <= k < half:
            relay_hidden(k)
        if k >= 2 and (k - 2) in RELAY:
            relay_piece(k - 2)
    def weight_of(k, first, final):
        if k == last:
            hid_load.wait()
            rows_in = disp[last]
        else:
            if k == last - 1 or k % 2 == 1:
                hid_recv[k].wait_recv()
            for cp in p_recv[k][1:] if k in RELAY else p_recv[k]:
                cp.wait_recv()
            rows_in = gath[k]
        weight_part(k, rows_in.reshape(slots, width), first, final)

    for k in range(last - 1, last):
        if k in RELAY:
            relay_piece(k)
    order = [0, last - 1, last] + list(range(1, last - 1))
    for at, k in enumerate(order):
        if k == last:
            finish_y(last)
        weight_of(k, at == 0, at == last)
    for cp in started:
        cp.wait_send()


def fused(sizes, out_grad, expert_ids, gate_weight, hidden_saved, down_weight):
    n_dp, n_ctx, n_tp, cap = sizes
    tokens, d_model = out_grad.shape
    width = d_model // n_dp
    rows = n_tp * cap
    slots, ff = hidden_saved.shape[2:]
    bf, dma = jnp.bfloat16, pltpu.SemaphoreType.DMA
    vmem, hbm = pl.BlockSpec(memory_space=pltpu.VMEM), pl.BlockSpec(memory_space=pl.ANY)
    hidden_grad, weight_grad = pl.pallas_call(
        functools.partial(kernel, sizes),
        out_shape=(
            jax.ShapeDtypeStruct((slots, ff), bf),
            jax.ShapeDtypeStruct((ff, width), bf),
        ),
        in_specs=[vmem, vmem, hbm, hbm, hbm],
        out_specs=(vmem, vmem),
        scratch_shapes=[
            pltpu.VMEM((n_dp, tokens, width), bf),
            pltpu.VMEM((n_dp, ff, width), bf),
            pltpu.VMEM((n_dp, rows, width), bf),
            pltpu.VMEM((n_dp, n_ctx, rows, width), bf),
            pltpu.VMEM((n_dp - 1, n_ctx, rows, width), bf),
            pltpu.VMEM((n_dp, slots, ff), bf),
            pltpu.VMEM((slots, ff), jnp.float32),
            pltpu.VMEM((ff, width), jnp.float32),
            dma((3, n_dp)),
            dma((n_dp, n_tp)),
            dma((n_dp, n_tp)),
            dma((n_dp, n_ctx)),
            dma((n_dp, n_ctx)),
            dma((n_dp, n_ctx)),
            dma((n_dp, n_ctx)),
            dma((n_dp,)),
            dma((n_dp,)),
        ],
        compiler_params=pltpu.CompilerParams(collective_id=0, has_side_effects=True),
    )(expert_ids.T, gate_weight.T, out_grad, hidden_saved[0, 0], down_weight[0])
    return hidden_grad[None, None], weight_grad[None]


def per_device(out_grad, expert_ids, gate_weight, hidden_saved, down_weight):
    n_dp, n_ctx, n_tp = (lax.axis_size(name) for name in ("dp", "ctx", "tp"))
    slots, ff = hidden_saved.shape[2:]
    cap = slots // (n_ctx * n_tp)
    args = (out_grad, expert_ids, gate_weight, hidden_saved, down_weight)
    tiled = cap % ROWS_PER_TILE == 0 and ff % LANES == 0 and n_dp % 2 == 0
    if tiled and out_grad.shape[1] % (n_dp * LANES) == 0:
        return fused((n_dp, n_ctx, n_tp, cap), *args)
    return plain(*args)


def solution(mesh):
    placed = (
        P(("dp", "ctx", "tp"), None),
        P(("dp", "ctx", "tp"), None),
        P(("dp", "ctx", "tp"), None),
        P("dp", "tp", None, "ctx"),
        P("tp", "ctx", None),
    )
    return jax.shard_map(
        per_device,
        mesh=mesh,
        in_specs=placed,
        out_specs=(P("dp", "tp", None, "ctx"), P("tp", "ctx", "dp")),
        check_vma=False,
    )
```

```python
import functools

import jax
import jax.numpy as jnp
from jax import lax
from jax.experimental import pallas as pl
from jax.experimental.pallas import tpu as pltpu
from jax.sharding import PartitionSpec as P

MESH = pl.DeviceIdType.MESH
RELAY = (1,)
DIRECT = (1, 2)
ROWS_PER_TILE = 16
LANES = 128


def plain(out_grad, expert_ids, gate_weight, hidden_saved, down_weight):
    experts = lax.axis_size("tp")
    width = out_grad.shape[1]
    slots_all = hidden_saved.shape[2]
    capacity = slots_all // (lax.axis_size("ctx") * experts)
    choice_rows = expert_ids[:, 0]
    onehot = (choice_rows[:, None] == jnp.arange(experts, dtype=jnp.int32)[None, :]).astype(
        jnp.int32
    )
    before = jnp.cumsum(onehot, axis=0) - onehot
    slot_index = jnp.sum(before * onehot, axis=1)
    target = jnp.arange(experts * capacity, dtype=jnp.int32)
    select = (
        (choice_rows[None, :] == (target // capacity)[:, None])
        & (slot_index[None, :] == (target % capacity)[:, None])
    ).astype(jnp.bfloat16)
    routed = (gate_weight * out_grad.astype(jnp.float32)).astype(jnp.bfloat16)
    outgoing = jnp.dot(select, routed, preferred_element_type=jnp.float32).astype(jnp.bfloat16)
    outgoing = outgoing.reshape(experts, capacity, width)
    incoming = lax.all_to_all(outgoing, "tp", split_axis=0, concat_axis=0, tiled=True)
    incoming = incoming.reshape(experts * capacity, width)
    group_rows = lax.all_gather(incoming, "ctx", axis=0, tiled=True)
    hidden_grad = jnp.einsum(
        "rd,fd->rf", group_rows, down_weight[0], preferred_element_type=jnp.float32
    )
    partial_value = jnp.einsum(
        "rf,rd->fd", hidden_saved[0, 0], group_rows, preferred_element_type=jnp.float32
    )
    rounded = lax.optimization_barrier(partial_value.astype(jnp.bfloat16)).astype(jnp.float32)
    summed = lax.psum_scatter(rounded.astype(jnp.bfloat16), "dp", scatter_dimension=1, tiled=True)
    return (hidden_grad.astype(jnp.bfloat16)[None, None], summed[None])


def kernel(
    sizes, ids_ref, gate_ref, og_hbm, hs_hbm, dw_hbm, hg_ref, wg_ref,
    ogb, wbuf, outb, disp, gath, hid, hgacc, wgacc, hg_buf, wg_buf, out_sem,
    load_sem, zs, zr, ys, yr, ps, pr, qs, qr, hs, hr,
):
    n_dp, n_ctx, n_tp, cap = sizes
    half = n_dp // 2
    rows = n_tp * cap
    width = ogb.shape[2]
    slots = n_ctx * rows
    ff = hid.shape[2]
    last = n_dp - 1
    r, c, t = lax.axis_index("dp"), lax.axis_index("ctx"), lax.axis_index("tp")
    hi, lo = r // 2, r % 2

    steps = [(a, b) for a in range(1, half) for b in (0, 1)] + [(0, 1), (0, 0)]

    def replica(a, b):
        return lax.rem(hi + a, half) * 2 + lax.rem(lo + b, 2)

    dest = [replica(a, b) for a, b in steps]

    og_loads, w_loads = [], []
    for k in range(n_dp):
        cols = pl.ds(pl.multiple_of(dest[k] * width, LANES), width)
        cp = pltpu.make_async_copy(og_hbm.at[:, cols], ogb.at[k], load_sem.at[0, k])
        cp.start()
        og_loads.append(cp)
    hid_load = pltpu.make_async_copy(hs_hbm, hid.at[last], load_sem.at[2, 0])
    hid_load.start()
    for k in range(n_dp):
        cols = pl.ds(pl.multiple_of(dest[k] * width, LANES), width)
        cp = pltpu.make_async_copy(dw_hbm.at[:, cols], wbuf.at[k], load_sem.at[1, k])
        cp.start()
        w_loads.append(cp)

    barrier = pltpu.get_barrier_semaphore()
    peers = [(r, c, lax.rem(t + d, n_tp)) for d in range(1, n_tp)]
    peers += [(r, lax.rem(c + d, n_ctx), t) for d in range(1, n_ctx)]
    peers += [(dest[k], c, t) for k in range(n_dp - 1)]
    for peer in peers:
        pl.semaphore_signal(barrier, inc=1, device_id=peer, device_id_type=MESH)

    tokens = ids_ref.shape[1]
    row = lax.broadcasted_iota(jnp.int32, (rows, tokens), 0)
    row_expert = row // cap
    row_slot = (row - row_expert * cap).astype(jnp.float32)
    onehot = jnp.where(ids_ref[...] == row_expert, 1.0, 0.0)
    earlier = (
        lax.broadcasted_iota(jnp.int32, (tokens, tokens), 0)
        < lax.broadcasted_iota(jnp.int32, (tokens, tokens), 1)
    )
    before = jnp.dot(
        onehot.astype(jnp.bfloat16),
        jnp.where(earlier, 1.0, 0.0).astype(jnp.bfloat16),
        preferred_element_type=jnp.float32,
    )
    select = jnp.where(before == row_slot, onehot, 0.0).astype(jnp.bfloat16)
    gate = jnp.broadcast_to(gate_ref[...], (tokens, tokens)).T[:, :1]

    started = []

    def send(src, dst, ssem, rsem, device):
        cp = pltpu.make_async_remote_copy(
            src_ref=src, dst_ref=dst, send_sem=ssem, recv_sem=rsem,
            device_id=device, device_id_type=MESH,
        )
        cp.start()
        started.append(cp)
        return cp

    y_recv = [[[] for _ in range(n_ctx)] for _ in range(n_dp)]

    def share(k, src, part, at):
        for d in range(1, n_ctx):
            to = lax.rem(c + n_ctx - d, n_ctx)
            y_recv[k][d].append(
                send(src, disp.at[k, c, part], ys.at[k, d, at], yr.at[k, d, at], (r, to, t))
            )

    hid_recv = [None] * n_dp
    pl.semaphore_wait(barrier, len(peers))
    for s in [2 * a for a in range(half - 1)] + [n_dp - 2]:
        hid_recv[s] = send(hs_hbm, hid.at[s], hs.at[s], hr.at[s], (dest[s], c, t))
    z_recv = []
    own_rows = pl.ds(pl.multiple_of(t * cap, cap), cap)
    for k in range(n_dp):
        og_loads[k].wait()
        routed = (gate * ogb[k].astype(jnp.float32)).astype(jnp.bfloat16)
        outb[k] = jnp.dot(select, routed, preferred_element_type=jnp.float32).astype(jnp.bfloat16)
        copies = []
        for d in range(1, n_tp):
            to = lax.rem(t + d, n_tp)
            src = outb.at[k, pl.ds(pl.multiple_of(to * cap, cap), cap)]
            copies.append(
                send(src, disp.at[k, c, own_rows], zs.at[k, d - 1], zr.at[k, d - 1], (r, c, to))
            )
        z_recv.append(copies)
        share(k, outb.at[k, own_rows], own_rows, 0)
        disp[k, c, own_rows, :] = outb[k, own_rows, :]

    out_copies, q_recv = [], []
    cut = rows * DIRECT[0] // DIRECT[1]
    p_recv = [[None] * n_ctx for _ in range(n_dp)]

    def relay_hidden(a):
        s = 2 * (a - 1)
        hid_recv[s].wait_recv()
        hid_recv[s + 1] = send(
            hid.at[s], hid.at[s + 1], hs.at[s + 1], hr.at[s + 1], (dest[n_dp - 2], c, t)
        )

    def hidden_part(k):
        w_loads[k].wait()
        part = lax.dot_general(
            disp[k].reshape(slots, width), wbuf[k], (((1,), (1,)), ((), ())),
            preferred_element_type=jnp.float32,
        )
        if k == 0:
            hgacc[...] = part
        elif k < last:
            hgacc[...] += part
        else:
            hg_buf[...] = (hgacc[...] + part).astype(hg_buf.dtype)
            out_copies.append(pltpu.make_async_copy(hg_buf, hg_ref, out_sem.at[0]))
            out_copies[-1].start()

    def weight_part(k, rows_in, first, final):
        tile = 256 if ff % 256 == 0 else LANES
        for f in range(0, ff, tile):
            part = lax.dot_general(
                hid[k, :, f : f + tile], rows_in, (((0,), (0,)), ((), ())),
                preferred_element_type=jnp.float32,
            )
            if not first:
                part = wgacc[f : f + tile, :] + part
            if final:
                wg_buf[f : f + tile, :] = part.astype(wg_buf.dtype)
                out_copies.append(
                    pltpu.make_async_copy(
                        wg_buf.at[f : f + tile], wg_ref.at[f : f + tile], out_sem.at[1 + f // tile]
                    )
                )
                out_copies[-1].start()
            else:
                wgacc[f : f + tile, :] = part

    def finish_y(k):
        for d in range(1, n_ctx):
            for cp in y_recv[k][d]:
                cp.wait_recv()
            if k < last:
                other = lax.rem(c + d, n_ctx)
                part = pl.ds(0, cut if k in RELAY else rows)
                p_recv[k][d] = send(
                    disp.at[k, other, part], gath.at[k, other, part], ps.at[k, d], pr.at[k, d],
                    (dest[k], c, t),
                )
        hidden_part(k)

    def relay_piece(k):
        p_recv[k][0].wait_recv()
        for d in range(1, n_ctx):
            to = lax.rem(c + n_ctx - d, n_ctx)
            part = pl.ds(cut, rows - cut)
            q_recv.append(
                send(
                    gath.at[k, c, part], gath.at[k, c, part], qs.at[k, d], qr.at[k, d], (r, to, t)
                )
            )

    for k in range(n_dp):
        for d in range(1, n_tp):
            z_recv[k][d - 1].wait_recv()
            source = lax.rem(t + n_tp - d, n_tp)
            part = pl.ds(pl.multiple_of(source * cap, cap), cap)
            share(k, disp.at[k, c, part], part, d)
        if k < last:
            p_recv[k][0] = send(
                disp.at[k, c], gath.at[k, c], ps.at[k, 0], pr.at[k, 0], (dest[k], c, t)
            )
        if k >= 1:
            finish_y(k - 1)
        if 1 <= k < half:
            relay_hidden(k)
        if k >= 2 and (k - 2) in RELAY:
            relay_piece(k - 2)
    def weight_of(k, first, final):
        if k == last:
            hid_load.wait()
            rows_in = disp[last]
        else:
            if k == last - 1 or k % 2 == 1:
                hid_recv[k].wait_recv()
            for cp in p_recv[k][1:] + q_recv if k in RELAY else p_recv[k]:
                cp.wait_recv()
            rows_in = gath[k]
        weight_part(k, rows_in.reshape(slots, width), first, final)

    for k in range(last - 1, last):
        if k in RELAY:
            relay_piece(k)
    order = [0, last - 1, last] + list(range(1, last - 1))
    for at, k in enumerate(order):
        if k == last:
            finish_y(last)
        weight_of(k, at == 0, at == last)
    for cp in started:
        cp.wait_send()
    for cp in out_copies:
        cp.wait()


def fused(sizes, out_grad, expert_ids, gate_weight, hidden_saved, down_weight):
    n_dp, n_ctx, n_tp, cap = sizes
    tokens, d_model = out_grad.shape
    width = d_model // n_dp
    rows = n_tp * cap
    slots, ff = hidden_saved.shape[2:]
    bf, dma = jnp.bfloat16, pltpu.SemaphoreType.DMA
    vmem, hbm = pl.BlockSpec(memory_space=pltpu.VMEM), pl.BlockSpec(memory_space=pl.ANY)
    hidden_grad, weight_grad = pl.pallas_call(
        functools.partial(kernel, sizes),
        out_shape=(
            jax.ShapeDtypeStruct((slots, ff), bf),
            jax.ShapeDtypeStruct((ff, width), bf),
        ),
        in_specs=[vmem, vmem, hbm, hbm, hbm],
        out_specs=(hbm, hbm),
        scratch_shapes=[
            pltpu.VMEM((n_dp, tokens, width), bf),
            pltpu.VMEM((n_dp, ff, width), bf),
            pltpu.VMEM((n_dp, rows, width), bf),
            pltpu.VMEM((n_dp, n_ctx, rows, width), bf),
            pltpu.VMEM((n_dp - 1, n_ctx, rows, width), bf),
            pltpu.VMEM((n_dp, slots, ff), bf),
            pltpu.VMEM((slots, ff), jnp.float32),
            pltpu.VMEM((ff, width), jnp.float32),
            pltpu.VMEM((slots, ff), bf),
            pltpu.VMEM((ff, width), bf),
            dma((1 + ff // LANES,)),
            dma((3, n_dp)),
            dma((n_dp, n_tp)),
            dma((n_dp, n_tp)),
            dma((n_dp, n_ctx, n_tp)),
            dma((n_dp, n_ctx, n_tp)),
            dma((n_dp, n_ctx)),
            dma((n_dp, n_ctx)),
            dma((n_dp, n_ctx)),
            dma((n_dp, n_ctx)),
            dma((n_dp,)),
            dma((n_dp,)),
        ],
        compiler_params=pltpu.CompilerParams(collective_id=0, has_side_effects=True),
    )(expert_ids.T, gate_weight.T, out_grad, hidden_saved[0, 0], down_weight[0])
    hidden_grad, weight_grad = settle(hidden_grad, weight_grad)
    return hidden_grad[None, None], weight_grad[None]


def settle_kernel(pieces, a_ref, b_ref, a_out, b_out, a_buf, b_buf, in_sem, out_sem):
    moves = [(a_ref, a_buf, a_out, 0, a_ref.shape[0])]
    size = b_ref.shape[0] // pieces
    moves += [(b_ref, b_buf, b_out, p * size, size) for p in range(pieces)]
    loads, stores = [], []
    for i, (src, buf, _, start, length) in enumerate(moves):
        part = pl.ds(start, length)
        loads.append(pltpu.make_async_copy(src.at[part], buf.at[part], in_sem.at[i]))
        loads[-1].start()
    for i, (_, buf, dst, start, length) in enumerate(moves):
        part = pl.ds(start, length)
        loads[i].wait()
        stores.append(pltpu.make_async_copy(buf.at[part], dst.at[part], out_sem.at[i]))
        stores[-1].start()
    for cp in stores:
        cp.wait()


def settle(a, b):
    pieces = 4 if b.shape[0] % (4 * ROWS_PER_TILE) == 0 else 1
    hbm = pl.BlockSpec(memory_space=pl.ANY)
    return pl.pallas_call(
        functools.partial(settle_kernel, pieces),
        out_shape=tuple(jax.ShapeDtypeStruct(x.shape, x.dtype) for x in (a, b)),
        in_specs=[hbm, hbm],
        out_specs=(hbm, hbm),
        scratch_shapes=[
            pltpu.VMEM(a.shape, a.dtype),
            pltpu.VMEM(b.shape, b.dtype),
            pltpu.SemaphoreType.DMA((pieces + 1,)),
            pltpu.SemaphoreType.DMA((pieces + 1,)),
        ],
    )(a, b)


def per_device(out_grad, expert_ids, gate_weight, hidden_saved, down_weight):
    n_dp, n_ctx, n_tp = (lax.axis_size(name) for name in ("dp", "ctx", "tp"))
    slots, ff = hidden_saved.shape[2:]
    cap = slots // (n_ctx * n_tp)
    args = (out_grad, expert_ids, gate_weight, hidden_saved, down_weight)
    tiled = cap % ROWS_PER_TILE == 0 and ff % LANES == 0 and n_dp % 2 == 0
    if tiled and out_grad.shape[1] % (n_dp * LANES) == 0:
        return fused((n_dp, n_ctx, n_tp, cap), *args)
    return plain(*args)


def solution(mesh):
    placed = (
        P(("dp", "ctx", "tp"), None),
        P(("dp", "ctx", "tp"), None),
        P(("dp", "ctx", "tp"), None),
        P("dp", "tp", None, "ctx"),
        P("tp", "ctx", None),
    )
    return jax.shard_map(
        per_device,
        mesh=mesh,
        in_specs=placed,
        out_specs=(P("dp", "tp", None, "ctx"), P("tp", "ctx", "dp")),
        check_vma=False,
    )
```

```python
import functools

import jax
import jax.numpy as jnp
from jax import lax
from jax.experimental import pallas as pl
from jax.experimental.pallas import tpu as pltpu
from jax.sharding import PartitionSpec as P

MESH = pl.DeviceIdType.MESH
RELAY = (1,)
DIRECT = (1, 2)
ROWS_PER_TILE = 16
LANES = 128


def plain(out_grad, expert_ids, gate_weight, hidden_saved, down_weight):
    experts = lax.axis_size("tp")
    width = out_grad.shape[1]
    slots_all = hidden_saved.shape[2]
    capacity = slots_all // (lax.axis_size("ctx") * experts)
    choice_rows = expert_ids[:, 0]
    onehot = (choice_rows[:, None] == jnp.arange(experts, dtype=jnp.int32)[None, :]).astype(
        jnp.int32
    )
    before = jnp.cumsum(onehot, axis=0) - onehot
    slot_index = jnp.sum(before * onehot, axis=1)
    target = jnp.arange(experts * capacity, dtype=jnp.int32)
    select = (
        (choice_rows[None, :] == (target // capacity)[:, None])
        & (slot_index[None, :] == (target % capacity)[:, None])
    ).astype(jnp.bfloat16)
    routed = (gate_weight * out_grad.astype(jnp.float32)).astype(jnp.bfloat16)
    outgoing = jnp.dot(select, routed, preferred_element_type=jnp.float32).astype(jnp.bfloat16)
    outgoing = outgoing.reshape(experts, capacity, width)
    incoming = lax.all_to_all(outgoing, "tp", split_axis=0, concat_axis=0, tiled=True)
    incoming = incoming.reshape(experts * capacity, width)
    group_rows = lax.all_gather(incoming, "ctx", axis=0, tiled=True)
    hidden_grad = jnp.einsum(
        "rd,fd->rf", group_rows, down_weight[0], preferred_element_type=jnp.float32
    )
    partial_value = jnp.einsum(
        "rf,rd->fd", hidden_saved[0, 0], group_rows, preferred_element_type=jnp.float32
    )
    rounded = lax.optimization_barrier(partial_value.astype(jnp.bfloat16)).astype(jnp.float32)
    summed = lax.psum_scatter(rounded.astype(jnp.bfloat16), "dp", scatter_dimension=1, tiled=True)
    return (hidden_grad.astype(jnp.bfloat16)[None, None], summed[None])


def kernel(
    sizes, ids_ref, gate_ref, og_hbm, hs_hbm, dw_hbm, hg_ref, wg_ref,
    ogb, wbuf, outb, disp, gath, hid, hgacc, wgacc, hg_buf, wg_buf, out_sem,
    load_sem, zs, zr, ys, yr, ps, pr, qs, qr, hs, hr, gs, gr,
):
    n_dp, n_ctx, n_tp, cap = sizes
    half = n_dp // 2
    rows = n_tp * cap
    width = ogb.shape[2]
    slots = n_ctx * rows
    ff = hid.shape[2]
    last = n_dp - 1
    r, c, t = lax.axis_index("dp"), lax.axis_index("ctx"), lax.axis_index("tp")
    hi, lo = r // 2, r % 2

    steps = [(a, b) for a in range(1, half) for b in (0, 1)] + [(0, 1), (0, 0)]

    def replica(a, b):
        return lax.rem(hi + a, half) * 2 + lax.rem(lo + b, 2)

    dest = [replica(a, b) for a, b in steps]

    og_loads, w_loads = [], []
    for k in range(n_dp):
        cols = pl.ds(pl.multiple_of(dest[k] * width, LANES), width)
        cp = pltpu.make_async_copy(og_hbm.at[:, cols], ogb.at[k], load_sem.at[0, k])
        cp.start()
        og_loads.append(cp)
    hid_load = pltpu.make_async_copy(hs_hbm, hid.at[last], load_sem.at[2, 0])
    hid_load.start()
    for k in range(n_dp):
        cols = pl.ds(pl.multiple_of(dest[k] * width, LANES), width)
        cp = pltpu.make_async_copy(dw_hbm.at[:, cols], wbuf.at[k], load_sem.at[1, k])
        cp.start()
        w_loads.append(cp)

    barrier = pltpu.get_barrier_semaphore()
    peers = [(r, c, lax.rem(t + d, n_tp)) for d in range(1, n_tp)]
    peers += [(r, lax.rem(c + d, n_ctx), t) for d in range(1, n_ctx)]
    peers += [(dest[k], c, t) for k in range(n_dp - 1)]
    for peer in peers:
        pl.semaphore_signal(barrier, inc=1, device_id=peer, device_id_type=MESH)

    tokens = ids_ref.shape[1]
    row = lax.broadcasted_iota(jnp.int32, (rows, tokens), 0)
    row_expert = row // cap
    row_slot = (row - row_expert * cap).astype(jnp.float32)
    onehot = jnp.where(ids_ref[...] == row_expert, 1.0, 0.0)
    earlier = (
        lax.broadcasted_iota(jnp.int32, (tokens, tokens), 0)
        < lax.broadcasted_iota(jnp.int32, (tokens, tokens), 1)
    )
    before = jnp.dot(
        onehot.astype(jnp.bfloat16),
        jnp.where(earlier, 1.0, 0.0).astype(jnp.bfloat16),
        preferred_element_type=jnp.float32,
    )
    select = jnp.where(before == row_slot, onehot, 0.0).astype(jnp.bfloat16)
    gate = jnp.broadcast_to(gate_ref[...], (tokens, tokens)).T[:, :1]

    started = []

    def send(src, dst, ssem, rsem, device):
        cp = pltpu.make_async_remote_copy(
            src_ref=src, dst_ref=dst, send_sem=ssem, recv_sem=rsem,
            device_id=device, device_id_type=MESH,
        )
        cp.start()
        started.append(cp)
        return cp

    y_recv = [[[] for _ in range(n_ctx)] for _ in range(n_dp)]

    def share(k, src, part, at):
        for d in range(1, n_ctx):
            to = lax.rem(c + n_ctx - d, n_ctx)
            y_recv[k][d].append(
                send(src, disp.at[k, c, part], ys.at[k, d, at], yr.at[k, d, at], (r, to, t))
            )

    g_recv = [[] for _ in range(n_dp)]

    def give(k, src, part, at):
        g_recv[k].append(
            send(src, gath.at[k, c, part], gs.at[k, at], gr.at[k, at], (dest[k], c, t))
        )

    hid_recv = [None] * n_dp
    pl.semaphore_wait(barrier, len(peers))
    for s in [2 * a for a in range(half - 1)] + [n_dp - 2]:
        hid_recv[s] = send(hs_hbm, hid.at[s], hs.at[s], hr.at[s], (dest[s], c, t))
    z_recv = []
    own_rows = pl.ds(pl.multiple_of(t * cap, cap), cap)
    for k in range(n_dp):
        og_loads[k].wait()
        routed = (gate * ogb[k].astype(jnp.float32)).astype(jnp.bfloat16)
        outb[k] = jnp.dot(select, routed, preferred_element_type=jnp.float32).astype(jnp.bfloat16)
        copies = []
        for d in range(1, n_tp):
            to = lax.rem(t + d, n_tp)
            src = outb.at[k, pl.ds(pl.multiple_of(to * cap, cap), cap)]
            copies.append(
                send(src, disp.at[k, c, own_rows], zs.at[k, d - 1], zr.at[k, d - 1], (r, c, to))
            )
        z_recv.append(copies)
        share(k, outb.at[k, own_rows], own_rows, 0)
        if k < last:
            give(k, outb.at[k, own_rows], own_rows, 0)
        disp[k, c, own_rows, :] = outb[k, own_rows, :]

    out_copies, q_recv = [], []
    cut = rows * DIRECT[0] // DIRECT[1]
    p_recv = [[None] * n_ctx for _ in range(n_dp)]

    def relay_hidden(a):
        s = 2 * (a - 1)
        hid_recv[s].wait_recv()
        hid_recv[s + 1] = send(
            hid.at[s], hid.at[s + 1], hs.at[s + 1], hr.at[s + 1], (dest[n_dp - 2], c, t)
        )

    def hidden_part(k):
        w_loads[k].wait()
        part = lax.dot_general(
            disp[k].reshape(slots, width), wbuf[k], (((1,), (1,)), ((), ())),
            preferred_element_type=jnp.float32,
        )
        if k == 0:
            hgacc[...] = part
        elif k < last:
            hgacc[...] += part
        else:
            hg_buf[...] = (hgacc[...] + part).astype(hg_buf.dtype)
            out_copies.append(pltpu.make_async_copy(hg_buf, hg_ref, out_sem.at[0]))
            out_copies[-1].start()

    def weight_part(k, rows_in, first, final):
        tile = 256 if ff % 256 == 0 else LANES
        for f in range(0, ff, tile):
            part = lax.dot_general(
                hid[k, :, f : f + tile], rows_in, (((0,), (0,)), ((), ())),
                preferred_element_type=jnp.float32,
            )
            if not first:
                part = wgacc[f : f + tile, :] + part
            if final:
                wg_buf[f : f + tile, :] = part.astype(wg_buf.dtype)
                out_copies.append(
                    pltpu.make_async_copy(
                        wg_buf.at[f : f + tile], wg_ref.at[f : f + tile], out_sem.at[1 + f // tile]
                    )
                )
                out_copies[-1].start()
            else:
                wgacc[f : f + tile, :] = part

    def finish_y(k):
        for d in range(1, n_ctx):
            for cp in y_recv[k][d]:
                cp.wait_recv()
            if k < last:
                other = lax.rem(c + d, n_ctx)
                part = pl.ds(0, cut if k in RELAY else rows)
                p_recv[k][d] = send(
                    disp.at[k, other, part], gath.at[k, other, part], ps.at[k, d], pr.at[k, d],
                    (dest[k], c, t),
                )
        hidden_part(k)

    def relay_piece(k):
        for cp in g_recv[k]:
            cp.wait_recv()
        for d in range(1, n_ctx):
            to = lax.rem(c + n_ctx - d, n_ctx)
            part = pl.ds(cut, rows - cut)
            q_recv.append(
                send(
                    gath.at[k, c, part], gath.at[k, c, part], qs.at[k, d], qr.at[k, d], (r, to, t)
                )
            )

    for k in range(n_dp):
        for d in range(1, n_tp):
            z_recv[k][d - 1].wait_recv()
            source = lax.rem(t + n_tp - d, n_tp)
            part = pl.ds(pl.multiple_of(source * cap, cap), cap)
            share(k, disp.at[k, c, part], part, d)
            if k < last:
                give(k, disp.at[k, c, part], part, d)
        if k >= 2 and (k - 2) in RELAY:
            relay_piece(k - 2)
        if k >= 1:
            finish_y(k - 1)
        if 1 <= k < half:
            relay_hidden(k)
    def weight_of(k, first, final):
        if k == last:
            hid_load.wait()
            rows_in = disp[last]
        else:
            if k == last - 1 or k % 2 == 1:
                hid_recv[k].wait_recv()
            extra = q_recv if k in RELAY else g_recv[k]
            for cp in p_recv[k][1:] + extra:
                cp.wait_recv()
            rows_in = gath[k]
        weight_part(k, rows_in.reshape(slots, width), first, final)

    for k in range(last - 1, last):
        if k in RELAY:
            relay_piece(k)
    order = [0, last - 1, last] + list(range(1, last - 1))
    for at, k in enumerate(order):
        if k == last:
            finish_y(last)
        weight_of(k, at == 0, at == last)
    for cp in started:
        cp.wait_send()
    for cp in out_copies:
        cp.wait()


def fused(sizes, out_grad, expert_ids, gate_weight, hidden_saved, down_weight):
    n_dp, n_ctx, n_tp, cap = sizes
    tokens, d_model = out_grad.shape
    width = d_model // n_dp
    rows = n_tp * cap
    slots, ff = hidden_saved.shape[2:]
    bf, dma = jnp.bfloat16, pltpu.SemaphoreType.DMA
    vmem, hbm = pl.BlockSpec(memory_space=pltpu.VMEM), pl.BlockSpec(memory_space=pl.ANY)
    hidden_grad, weight_grad = pl.pallas_call(
        functools.partial(kernel, sizes),
        out_shape=(
            jax.ShapeDtypeStruct((slots, ff), bf),
            jax.ShapeDtypeStruct((ff, width), bf),
        ),
        in_specs=[vmem, vmem, hbm, hbm, hbm],
        out_specs=(hbm, hbm),
        scratch_shapes=[
            pltpu.VMEM((n_dp, tokens, width), bf),
            pltpu.VMEM((n_dp, ff, width), bf),
            pltpu.VMEM((n_dp, rows, width), bf),
            pltpu.VMEM((n_dp, n_ctx, rows, width), bf),
            pltpu.VMEM((n_dp - 1, n_ctx, rows, width), bf),
            pltpu.VMEM((n_dp, slots, ff), bf),
            pltpu.VMEM((slots, ff), jnp.float32),
            pltpu.VMEM((ff, width), jnp.float32),
            pltpu.VMEM((slots, ff), bf),
            pltpu.VMEM((ff, width), bf),
            dma((1 + ff // LANES,)),
            dma((3, n_dp)),
            dma((n_dp, n_tp)),
            dma((n_dp, n_tp)),
            dma((n_dp, n_ctx, n_tp)),
            dma((n_dp, n_ctx, n_tp)),
            dma((n_dp, n_ctx)),
            dma((n_dp, n_ctx)),
            dma((n_dp, n_ctx)),
            dma((n_dp, n_ctx)),
            dma((n_dp,)),
            dma((n_dp,)),
            dma((n_dp, n_tp)),
            dma((n_dp, n_tp)),
        ],
        compiler_params=pltpu.CompilerParams(collective_id=0, has_side_effects=True),
    )(expert_ids.T, gate_weight.T, out_grad, hidden_saved[0, 0], down_weight[0])
    hidden_grad, weight_grad = settle(hidden_grad, weight_grad)
    return hidden_grad[None, None], weight_grad[None]


def settle_kernel(pieces, a_ref, b_ref, a_out, b_out, a_buf, b_buf, in_sem, out_sem):
    moves = [(a_ref, a_buf, a_out, 0, a_ref.shape[0])]
    size = b_ref.shape[0] // pieces
    moves += [(b_ref, b_buf, b_out, p * size, size) for p in range(pieces)]
    loads, stores = [], []
    for i, (src, buf, _, start, length) in enumerate(moves):
        part = pl.ds(start, length)
        loads.append(pltpu.make_async_copy(src.at[part], buf.at[part], in_sem.at[i]))
        loads[-1].start()
    for i, (_, buf, dst, start, length) in enumerate(moves):
        part = pl.ds(start, length)
        loads[i].wait()
        stores.append(pltpu.make_async_copy(buf.at[part], dst.at[part], out_sem.at[i]))
        stores[-1].start()
    for cp in stores:
        cp.wait()


def settle(a, b):
    pieces = 4 if b.shape[0] % (4 * ROWS_PER_TILE) == 0 else 1
    hbm = pl.BlockSpec(memory_space=pl.ANY)
    return pl.pallas_call(
        functools.partial(settle_kernel, pieces),
        out_shape=tuple(jax.ShapeDtypeStruct(x.shape, x.dtype) for x in (a, b)),
        in_specs=[hbm, hbm],
        out_specs=(hbm, hbm),
        scratch_shapes=[
            pltpu.VMEM(a.shape, a.dtype),
            pltpu.VMEM(b.shape, b.dtype),
            pltpu.SemaphoreType.DMA((pieces + 1,)),
            pltpu.SemaphoreType.DMA((pieces + 1,)),
        ],
    )(a, b)


def per_device(out_grad, expert_ids, gate_weight, hidden_saved, down_weight):
    n_dp, n_ctx, n_tp = (lax.axis_size(name) for name in ("dp", "ctx", "tp"))
    slots, ff = hidden_saved.shape[2:]
    cap = slots // (n_ctx * n_tp)
    args = (out_grad, expert_ids, gate_weight, hidden_saved, down_weight)
    tiled = cap % ROWS_PER_TILE == 0 and ff % LANES == 0 and n_dp % 2 == 0
    if tiled and out_grad.shape[1] % (n_dp * LANES) == 0:
        return fused((n_dp, n_ctx, n_tp, cap), *args)
    return plain(*args)


def solution(mesh):
    placed = (
        P(("dp", "ctx", "tp"), None),
        P(("dp", "ctx", "tp"), None),
        P(("dp", "ctx", "tp"), None),
        P("dp", "tp", None, "ctx"),
        P("tp", "ctx", None),
    )
    return jax.shard_map(
        per_device,
        mesh=mesh,
        in_specs=placed,
        out_specs=(P("dp", "tp", None, "ctx"), P("tp", "ctx", "dp")),
        check_vma=False,
    )
```
